256 devices in a mesh: gx: 32 (over y, z), gy: 8 (over x, core).
Axes of the slice: x: 4, y: 4, z: 8, core: 2. Of those that a mesh axis runs over, the one named last changes fastest.
Arguments:
- densities: bfloat16 [24576, 32, 128], P(('gx', 'gy')), may hold values from -6 to 6
- geometry: float32 [24576, 7, 128], P(('gx', 'gy')), as said below
- near_ids: int32 [24576, 8], P(('gx', 'gy')), may hold values from 0 to 24575, as said below
- basis_in: bfloat16 [24576, 64, 128], P(('gx', 'gy')), may hold values from -0.5 to 0.5
- basis_out: bfloat16 [24576, 64, 128], P(('gx', 'gy')), may hold values from -0.75 to 0.75
- leaf_up: bfloat16 [24576, 64, 64], P(('gx', 'gy')), may hold values from -0.078125 to 0.078125
- leaf_down: bfloat16 [24576, 64, 64], P(('gx', 'gy')), may hold values from -0.75 to 0.75
- leaf_coupling: bfloat16 [24576, 6, 64, 64], P(('gx', 'gy')), may hold values from -0.3125 to 0.3125
- leaf_far: int32 [24576, 6], P(('gx', 'gy')), may hold values from 0 to 24575, as said below
- leaf_count: int32 [24576], P(('gx', 'gy')), may hold values from 1 to 6, as said below
- cluster_up: bfloat16 [256, 64, 64], P(('gx', 'gy')), may hold values from -0.25 to 0.25
- cluster_down: bfloat16 [256, 64, 64], P(('gx', 'gy')), may hold values from -0.75 to 0.75
- cluster_coupling: bfloat16 [256, 6, 64, 64], P(('gx', 'gy')), may hold values from -0.3125 to 0.3125
- cluster_far: int32 [256, 6], P(('gx', 'gy')), may hold values from 0 to 255, as said below
- group_up: bfloat16 [32, 64, 64], replicated, may hold values from -0.375 to 0.375
- group_down: bfloat16 [32, 64, 64], P('gx'), may hold values from -0.75 to 0.75
- group_coupling: bfloat16 [32, 6, 64, 64], P('gx'), may hold values from -0.3125 to 0.3125
- group_far: int32 [32, 6], P('gx'), may hold values from 0 to 31, as said below
- root_coupling: bfloat16 [8, 8, 64, 64], replicated, may hold values from -0.25 to 0.25
Outputs:
- potential: float32 [24576, 32, 128], P(('gx', 'gy'))
The draws below stay inside these ranges and needn't reach their ends.
Inputs may be any that keep to these rules, and one draw needn't show every extreme that they name: `near_ids`: row l names 8 different leaves of a window of 9 consecutive leaves that contains l, centred on l where the ends allow. `leaf_far`: row l names 6 different leaves held by l's device or its two neighbours in leaf order, none within 4 leaves of l; only the first leaf_count[l] entries are used. `leaf_count`: every device holds a leaf with 6. `cluster_far`: row u names 6 different level-two clusters other than u, of u's group or the two groups beside it. `group_far`: row g names 6 different level-one clusters other than g. `geometry`: rows 0 to 2 hold a panel's centre, rows 3 to 5 its unit normal, row 6 its area, from 0.25 to 2.
All inputs are finite; a program needn't handle non-finite values.
Results may differ from the reference program's by a relative error of at most 0.012.
Values may be sent and summed in bfloat16 or wider, within the bound.
A program may use at most 128 MiB of HBM per device.

```python
import math
import jax
import jax.numpy as jnp
from jax import lax

LEAF_DEV = 96
M = 128
K = 64
R = 32
NF3 = 6
NN = 8
NF2 = 6
NF1 = 6
REACH = 4
BRANCH = 4
GROUP_SIZE = 8
GROUPS = 32
CLUSTERS = 256
ROOTS = 8
LEAVES = 24576


def pick_distinct(key, candidates, usable, wanted):
    pool_size = candidates.shape[1]
    column = lax.broadcasted_iota(jnp.int32, candidates.shape, 1)
    scores = jax.random.randint(key, candidates.shape, 0, 1 << 16) * (2 * pool_size) + column + pool_size
    scores = jnp.where(usable, scores, column)
    chosen = lax.top_k(scores, wanted)[1]
    return jnp.take_along_axis(candidates, chosen, axis=1).astype(jnp.int32)


def draw_near_ids(key, part):
    shape = (LEAVES, 2 * REACH + 1)
    leaf_index = lax.broadcasted_iota(jnp.int32, shape, 0)
    column = lax.broadcasted_iota(jnp.int32, shape, 1)
    window_start = jnp.clip(leaf_index - REACH, 0, LEAVES - 2 * REACH - 1)
    candidates = window_start + column
    return pick_distinct(jax.random.fold_in(key, 11), candidates, candidates >= 0, NN)


def draw_leaf_far(key, part):
    shape = (LEAVES, 3 * LEAF_DEV)
    leaf_index = lax.broadcasted_iota(jnp.int32, shape, 0)
    column = lax.broadcasted_iota(jnp.int32, shape, 1)
    candidates = (leaf_index // LEAF_DEV - 1) * LEAF_DEV + column
    usable = (candidates >= 0) & (candidates < LEAVES) & (jnp.abs(candidates - leaf_index) > REACH)
    return pick_distinct(jax.random.fold_in(key, 12), candidates, usable, NF3)


def draw_leaf_count(key, part):
    subkeys = jax.random.split(jax.random.fold_in(key, 13), 3)
    busy_level = jax.random.randint(subkeys[0], (CLUSTERS, 1), 1, NF3 + 1)
    counts = jax.random.randint(subkeys[1], (CLUSTERS, LEAF_DEV), 0, 1 << 16) % busy_level + 1
    full_slot = jax.random.randint(subkeys[2], (CLUSTERS, 1), 0, LEAF_DEV)
    column = lax.broadcasted_iota(jnp.int32, (CLUSTERS, LEAF_DEV), 1)
    counts = jnp.where(column == full_slot, NF3, counts)
    return counts.reshape(LEAVES).astype(jnp.int32)


def draw_cluster_far(key, part):
    shape = (CLUSTERS, 3 * GROUP_SIZE)
    cluster_index = lax.broadcasted_iota(jnp.int32, shape, 0)
    column = lax.broadcasted_iota(jnp.int32, shape, 1)
    candidates = (cluster_index // GROUP_SIZE - 1) * GROUP_SIZE + column
    usable = (candidates >= 0) & (candidates < CLUSTERS) & (candidates != cluster_index)
    return pick_distinct(jax.random.fold_in(key, 14), candidates, usable, NF2)


def draw_group_far(key, part):
    shape = (GROUPS, GROUPS)
    group_index = lax.broadcasted_iota(jnp.int32, shape, 0)
    candidates = lax.broadcasted_iota(jnp.int32, shape, 1)
    return pick_distinct(jax.random.fold_in(key, 15), candidates, candidates != group_index, NF1)


def draw_geometry(key, part):
    subkeys = jax.random.split(jax.random.fold_in(key, 17), 4)
    walk_steps = jax.random.normal(subkeys[0], (LEAVES, 3, 1), jnp.float32) * 0.15
    centre = jnp.cumsum(walk_steps, axis=0)
    spread_out = jax.random.normal(subkeys[1], (LEAVES, 3, M), jnp.float32) * 0.5
    panel_area = jnp.exp(jax.random.uniform(subkeys[3], (LEAVES, 1, M), jnp.float32, math.log(0.25), math.log(2.0)))
    direction = jax.random.normal(subkeys[2], (LEAVES, 3, M), jnp.float32)
    unit_normal = direction / jnp.sqrt(jnp.sum(direction * direction, axis=1, keepdims=True) + 1e-06)
    return jnp.concatenate([centre + spread_out, unit_normal, panel_area], axis=1).astype(jnp.float32)


def level_of(rng, dims, cuts, low, high):
    factor_of, own = 1.0, jax.random.fold_in(rng, 6)
    for position, blocks in cuts:
        heights = jnp.exp(jax.random.uniform(jax.random.fold_in(own, position), (blocks,), jnp.float32, low / len(cuts), high / len(cuts)))
        factor_of = factor_of * jnp.repeat(heights, dims[position] // blocks).reshape([-1 if axis == position else 1 for axis in range(len(dims))])
    return factor_of


def scatter_about(stream_key, dims, scale, reach, cuts=(), kind=jnp.bfloat16):
    factor_of = level_of(stream_key, dims, cuts, -0.22, 0.18) if cuts else 1.0
    entries = jax.random.normal(stream_key, dims, jnp.float32) * scale * factor_of
    return jnp.minimum(jnp.maximum(entries, -reach), reach).astype(kind)


def setup_inputs(seed: int = 0) -> dict:
    seeds = jax.random.split(jax.random.key(seed), 20)
    densities = scatter_about(seeds[0], (LEAVES, R, M), 1.0, 6.0, ((0, 256),))
    geometry = draw_geometry(jax.random.fold_in(seeds[19], 71), 0)
    near_ids = draw_near_ids(jax.random.fold_in(seeds[19], 71), 0)
    basis_in = scatter_about(seeds[3], (LEAVES, K, M), M ** -0.5, 0.5, ((0, 256),))
    basis_out = scatter_about(seeds[4], (LEAVES, K, M), K ** -0.5, 0.75, ((0, 256),))
    leaf_up = scatter_about(seeds[5], (LEAVES, K, K), (K * LEAF_DEV) ** -0.5, 0.078125, ((0, 256),))
    leaf_down = scatter_about(seeds[6], (LEAVES, K, K), K ** -0.5, 0.75, ((0, 256),))
    leaf_coupling = scatter_about(seeds[7], (LEAVES, NF3, K, K), (K * NF3) ** -0.5, 0.3125, ((0, 256),))
    leaf_far = draw_leaf_far(jax.random.fold_in(seeds[19], 71), 0)
    leaf_count = draw_leaf_count(jax.random.fold_in(seeds[19], 71), 0)
    cluster_up = scatter_about(seeds[10], (CLUSTERS, K, K), (K * GROUP_SIZE) ** -0.5, 0.25, ((0, 256),))
    cluster_down = scatter_about(seeds[11], (CLUSTERS, K, K), K ** -0.5, 0.75, ((0, 256),))
    cluster_coupling = scatter_about(seeds[12], (CLUSTERS, NF2, K, K), (K * NF2) ** -0.5, 0.3125, ((0, 256),))
    cluster_far = draw_cluster_far(jax.random.fold_in(seeds[19], 71), 0)
    group_up = scatter_about(seeds[14], (GROUPS, K, K), (K * BRANCH) ** -0.5, 0.375)
    group_down = scatter_about(seeds[15], (GROUPS, K, K), K ** -0.5, 0.75, ((0, 32),))
    group_coupling = scatter_about(seeds[16], (GROUPS, NF1, K, K), (K * NF1) ** -0.5, 0.3125, ((0, 32),))
    group_far = draw_group_far(jax.random.fold_in(seeds[19], 71), 0)
    root_coupling = scatter_about(seeds[18], (ROOTS, ROOTS, K, K), (K * ROOTS) ** -0.5, 0.25)
    return {"densities": densities, "geometry": geometry, "near_ids": near_ids, "basis_in": basis_in, "basis_out": basis_out, "leaf_up": leaf_up, "leaf_down": leaf_down, "leaf_coupling": leaf_coupling, "leaf_far": leaf_far, "leaf_count": leaf_count, "cluster_up": cluster_up, "cluster_down": cluster_down, "cluster_coupling": cluster_coupling, "cluster_far": cluster_far, "group_up": group_up, "group_down": group_down, "group_coupling": group_coupling, "group_far": group_far, "root_coupling": root_coupling}


four_pi = 4.0 * math.pi
leaf_block = 8

def rounded(value):
    return lax.optimization_barrier(value.astype(jnp.bfloat16)).astype(jnp.float32)

def near_kernel(target, source):
    offsets = [target[:, coord_id, :, None, None] - source[:, None, :, coord_id, :] for coord_id in range(3)]
    distance = offsets[0] * offsets[0] + offsets[1] * offsets[1] + offsets[2] * offsets[2]
    facing = source[:, None, :, 3, :] * offsets[0] + source[:, None, :, 4, :] * offsets[1] + source[:, None, :, 5, :] * offsets[2]
    panel_area = source[:, None, :, 6, :]
    spread = distance + panel_area
    return panel_area * facing / (four_pi * spread * jnp.sqrt(spread))

def cluster_view(array):
    return array.reshape((CLUSTERS, LEAF_DEV) + array.shape[1:])

def reference(densities, geometry, near_ids, basis_in, basis_out, leaf_up, leaf_down, leaf_coupling, leaf_far, leaf_count, cluster_up, cluster_down, cluster_coupling, cluster_far, group_up, group_down, group_coupling, group_far, root_coupling):
    wide = jnp.float32
    coeff_order = basis_in.shape[1]
    columns = densities.shape[1]

    def upward(operands):
        basis, values, lifting = operands
        coeffs = rounded(jnp.einsum('lkm,lrm->lkr', basis.astype(wide), values.astype(wide)))
        parent = rounded(jnp.einsum('lik,lkr->ir', lifting.astype(wide), coeffs))
        return (coeffs, parent)
    leaf_coeffs, cluster_coeffs = lax.map(upward, (cluster_view(basis_in), cluster_view(densities), cluster_view(leaf_up)))
    leaf_coeffs = leaf_coeffs.reshape(LEAVES, coeff_order, columns)
    cluster_terms = jnp.einsum('uik,ukr->uir', cluster_up.astype(wide), cluster_coeffs)
    group_coeffs = rounded(lax.optimization_barrier(jnp.sum(cluster_terms.reshape(GROUPS, GROUP_SIZE, coeff_order, columns), axis=1)))
    root_terms = jnp.einsum('gik,gkr->gir', group_up.astype(wide), group_coeffs)
    root_coeffs = rounded(lax.optimization_barrier(jnp.sum(root_terms.reshape(ROOTS, BRANCH, coeff_order, columns), axis=1)))
    root_field = rounded(jnp.einsum('qsik,skr->qir', root_coupling.astype(wide), root_coeffs))
    group_field = rounded(jnp.einsum('gfik,gfkr->gir', group_coupling.astype(wide), group_coeffs[group_far]) + jnp.einsum('gik,gkr->gir', group_down.astype(wide), jnp.repeat(root_field, BRANCH, axis=0)))
    cluster_field = rounded(jnp.einsum('ufik,ufkr->uir', cluster_coupling.astype(wide), cluster_coeffs[cluster_far]) + jnp.einsum('uik,ukr->uir', cluster_down.astype(wide), jnp.repeat(group_field, GROUP_SIZE, axis=0)))

    def downward(operands):
        lowering, coupling, partners, counts, basis, parent_field, target_geo, near_list = operands
        picked = leaf_coeffs[partners]
        live_mask = (lax.broadcasted_iota(jnp.int32, partners.shape, 1) < counts[:, None]).astype(wide)
        leaf_field = rounded(jnp.einsum('lfik,lfkr->lir', coupling.astype(wide), picked * live_mask[:, :, None, None]) + jnp.einsum('lik,kr->lir', lowering.astype(wide), parent_field))
        far_part = jnp.einsum('lkr,lkm->lrm', leaf_field, basis.astype(wide))

        def near_block(pieces):
            target, indices = pieces
            kernel = rounded(near_kernel(target, geometry[indices]))
            return jnp.einsum('bmnj,bnrj->brm', kernel, densities[indices].astype(wide))
        near_part = lax.map(near_block, (target_geo.reshape(LEAF_DEV // leaf_block, leaf_block, 7, -1), near_list.reshape(LEAF_DEV // leaf_block, leaf_block, -1)))
        return far_part + near_part.reshape(far_part.shape)
    potential = lax.map(downward, (cluster_view(leaf_down), cluster_view(leaf_coupling), cluster_view(leaf_far), cluster_view(leaf_count), cluster_view(basis_out), cluster_field, cluster_view(geometry), cluster_view(near_ids)))
    return potential.reshape(LEAVES, columns, -1)
```

```python
import functools
import math

import jax
import jax.numpy as jnp
from jax import lax
from jax.experimental import pallas as pl
from jax.experimental.pallas import tpu as pltpu
from jax.sharding import PartitionSpec as P

f32 = jnp.float32
bf16 = jnp.bfloat16
MESH = pl.DeviceIdType.MESH
NT = (((1,), (1,)), ((), ()))

REACH = 4
BRANCH = 4
HALO = 8
SPITCH = 65
TPITCH = 33
RPITCH = 97
FAR_LIMIT = 4096.0


def nt(a, b):
    return lax.dot_general(a, b, NT, preferred_element_type=f32)


def mm(a, b):
    return jnp.dot(a, b, preferred_element_type=f32)


def eye(n):
    rows = lax.broadcasted_iota(jnp.int32, (n, n), 0)
    cols = lax.broadcasted_iota(jnp.int32, (n, n), 1)
    return jnp.where(rows == cols, 1.0, 0.0).astype(bf16)


def split3(x):
    high = x.astype(bf16).astype(f32)
    rest = x - high
    mid = rest.astype(bf16).astype(f32)
    return high, mid, rest - mid


def low_lanes(shape):
    return lax.broadcasted_iota(jnp.int32, shape, len(shape) - 1) < 64


def fold(x):
    return jnp.concatenate([x[:16], x[16:]], axis=1)


def unfold(x):
    return jnp.concatenate([x[:, :64], x[:, 64:]], axis=0)


def slot_of(near_id, first, leaves):
    s = near_id - first
    s = jnp.where(s < 0, s + leaves + HALO, jnp.where(s < leaves, s, s + HALO))
    return jnp.clip(s, 0, leaves + 2 * HALO - 1)


def prepare(geo, rows, base, origin, src, tgt):
    u = [geo[k] - origin[k] for k in range(3)]
    area = geo[6]
    weight = area * (1.0 / (4.0 * math.pi))
    m = [geo[3 + k] * weight for k in range(3)]
    norm = u[0] * u[0] + u[1] * u[1] + u[2] * u[2]
    shift = -(m[0] * u[0] + m[1] * u[1] + m[2] * u[2])
    one = jnp.ones_like(norm)
    zero = jnp.zeros_like(norm)
    us = [split3(x) for x in u]
    vs = [tuple(-2.0 * y for y in x) for x in us]
    ms = [split3(x) for x in m]

    def put(ref, pitch, row, val):
        ref[pl.ds(base * pitch + row, rows, pitch), :] = val

    row = 0
    for k in range(3):
        for i, j in ((0, 0), (0, 1), (1, 0), (0, 2), (2, 0), (1, 1)):
            put(src, SPITCH, row, vs[k][i])
            put(src, SPITCH, 32 + row, ms[k][i])
            if tgt is not None:
                put(tgt, TPITCH, row, us[k][j])
            row += 1
    norms, totals, shifts = split3(norm), split3(norm + area), split3(shift)
    for i in range(3):
        put(src, SPITCH, row, one)
        put(src, SPITCH, 32 + row, zero)
        if tgt is not None:
            put(tgt, TPITCH, row, norms[i])
        row += 1
    for i in range(3):
        put(src, SPITCH, row, totals[i])
        put(src, SPITCH, 32 + row, shifts[i])
        if tgt is not None:
            put(tgt, TPITCH, row, one)
        row += 1
    for r in range(row, 32):
        put(src, SPITCH, r, zero)
        put(src, SPITCH, 32 + r, zero)
        if tgt is not None:
            put(tgt, TPITCH, r, zero)
    return jnp.max(norm)


def up_kernel(
    nx, ny, leaves,
    geo, ids, cluster_far, group_far, dens_hbm, basis_hbm, up, down, cluster_up, cluster_down, cluster_coupling,
    group_up, group_down, group_coupling, root_hbm,
    near_out, lift_out, coeff_out, mid_out, extent_out, dens_halo_out, geo_halo_out,
    dens, basis, geo_halo, src, tgt, sq, relay, lift, coeff, mid_all, term_all, top_all, root_row, near,
    in_sem, out_sem, halo_send, halo_recv, coeff_send, coeff_recv, mid_send, mid_recv, term_send, term_recv,
    top_send, top_recv,
):
    gx = lax.axis_index("gx")
    gy = lax.axis_index("gy")
    first = (gx * ny + gy) * leaves
    pairs = leaves // 2
    next_x = lax.rem(gx + 1, nx)
    prev_x = lax.rem(gx + nx - 1, nx)
    right = (jnp.where(gy == ny - 1, next_x, gx), lax.rem(gy + 1, ny))
    left = (jnp.where(gy == 0, prev_x, gx), lax.rem(gy + ny - 1, ny))

    loads = [
        pltpu.make_async_copy(dens_hbm, dens.at[pl.ds(0, leaves)], in_sem.at[0]),
        pltpu.make_async_copy(basis_hbm, basis, in_sem.at[1]),
        pltpu.make_async_copy(root_hbm.at[gx // BRANCH], root_row, in_sem.at[2]),
    ]
    for c in loads:
        c.start()

    barrier = pltpu.get_barrier_semaphore()

    def greet_x(k, c):
        pl.semaphore_signal(barrier, inc=1, device_id=(lax.rem(gx + k, nx), gy), device_id_type=MESH)
        return c

    def greet_y(k, c):
        other = lax.rem(gy + k, ny)
        for x in (prev_x, gx, next_x):
            pl.semaphore_signal(barrier, inc=1, device_id=(x, other), device_id_type=MESH)
        return c

    lax.fori_loop(1, nx, greet_x, 0)
    lax.fori_loop(1, ny, greet_y, 0)

    origin = [jnp.mean(geo[k, leaves // 2 : leaves // 2 + 1, :], axis=1, keepdims=True) for k in range(3)]
    extent = prepare(geo, leaves, 0, origin, src, tgt)

    ident = eye(leaves)

    def relayout(h, c):
        i = 2 * h
        x = jnp.concatenate([down[i], up[i], down[i + 1], up[i + 1]], axis=0)
        y = nt(ident, x)
        relay[pl.ds(i * RPITCH, leaves), :] = y[:, :128]
        relay[pl.ds((i + 1) * RPITCH, leaves), :] = y[:, 128:]
        return c

    lax.fori_loop(0, 32, relayout, 0, unroll=4)

    pl.semaphore_wait(barrier, (nx - 1) + 3 * (ny - 1))
    loads[0].wait()
    halo = []
    for side, (dest, leaf0, row0) in enumerate(
        ((right, leaves - REACH, leaves + HALO - REACH), (left, 0, leaves + HALO))
    ):
        halo.append(
            pltpu.make_async_remote_copy(
                src_ref=dens.at[pl.ds(leaf0, REACH)],
                dst_ref=dens.at[pl.ds(row0, REACH)],
                send_sem=halo_send.at[2 * side],
                recv_sem=halo_recv.at[2 * side],
                device_id=dest,
                device_id_type=MESH,
            )
        )
        halo.append(
            pltpu.make_async_remote_copy(
                src_ref=geo.at[:, pl.ds((leaves - HALO) * (1 - side), HALO), :],
                dst_ref=geo_halo.at[side],
                send_sem=halo_send.at[2 * side + 1],
                recv_sem=halo_recv.at[2 * side + 1],
                device_id=dest,
                device_id_type=MESH,
            )
        )
    for c in halo:
        c.start()

    loads[1].wait()
    low = low_lanes((32, 128))

    def upward(p, acc):
        x = dens[pl.ds(2 * p, 2)].reshape(64, 128)
        w = basis[pl.ds(2 * p, 2)].reshape(128, 128)
        y = nt(x, w)
        tile = jnp.where(low, y[:32], y[32:])
        coeff[p] = tile.astype(bf16)
        turned = pltpu.roll(tile, 64, 1)
        lhs = jnp.concatenate([jnp.where(low, 0.0, turned), jnp.where(low, 0.0, tile)], axis=1).astype(bf16)
        mats = []
        for b in range(2):
            mat = relay[pl.ds(2 * p + b, 64, RPITCH), :].astype(bf16)
            lift[2 * p + b] = mat
            mats.append(mat)
        return acc + nt(lhs, jnp.concatenate(mats, axis=1))

    mid = lax.fori_loop(0, pairs, upward, jnp.zeros((32, 64), f32), unroll=4)
    mid = mid.astype(bf16)
    term = nt(mid, cluster_up[0])
    mid_all[ny + gy] = fold(mid.astype(f32)).astype(bf16)
    term_all[gy] = fold(term)

    def term_copy(k):
        other = lax.rem(gy + k, ny)
        return pltpu.make_async_remote_copy(
            src_ref=term_all.at[gy], dst_ref=term_all.at[gy], send_sem=term_send.at[k], recv_sem=term_recv.at[gy],
            device_id=(gx, other), device_id_type=MESH,
        )

    def mid_copy(g, k):
        other = lax.rem(gy + k, ny)
        x = (next_x, gx, prev_x)[g]
        return pltpu.make_async_remote_copy(
            src_ref=mid_all.at[ny + gy], dst_ref=mid_all.at[g * ny + gy], send_sem=mid_send.at[g, k],
            recv_sem=mid_recv.at[g * ny + gy], device_id=(x, other), device_id_type=MESH,
        )

    def top_copy(k):
        return pltpu.make_async_remote_copy(
            src_ref=top_all.at[gx], dst_ref=top_all.at[gx], send_sem=top_send.at[k], recv_sem=top_recv.at[gx],
            device_id=(lax.rem(gx + k, nx), gy), device_id_type=MESH,
        )

    def coeff_copy(side):
        dest = (right, left)[side]
        return pltpu.make_async_remote_copy(
            src_ref=coeff, dst_ref=coeff_out.at[2 * side], send_sem=coeff_send.at[side], recv_sem=coeff_recv.at[side],
            device_id=dest, device_id_type=MESH,
        )

    def start_terms(k, c):
        term_copy(k).start()
        return c

    def start_mids(k, c):
        for g in range(3):
            mid_copy(g, k).start()
        return c

    lax.fori_loop(1, ny, start_terms, 0)
    mid_copy(0, 0).start()
    mid_copy(2, 0).start()
    lax.fori_loop(1, ny, start_mids, 0)

    for c in halo:
        c.wait()
    for side in range(2):
        extent = jnp.maximum(
            extent, prepare(geo_halo.at[side], HALO, leaves + HALO * side, origin, src, None)
        )
    extent_out[...] = jnp.full(extent_out.shape, extent, f32)

    turn = eye(128)

    def transpose(s, c):
        x = src[pl.ds(s * SPITCH, 64), :].astype(bf16)
        sq[s] = nt(turn, x).astype(bf16)
        return c

    lax.fori_loop(0, leaves + 2 * HALO, transpose, 0, unroll=4)
    zero = jnp.zeros((32, 128), bf16)

    def near_leaf(l, c):
        t = tgt[pl.ds(l * TPITCH, 32), :].astype(bf16)
        w = jnp.concatenate([jnp.concatenate([t, zero], 1), jnp.concatenate([zero, t], 1)], 0)
        kernels, values = [], []
        for n in range(8):
            s = slot_of(ids[n, l], first, leaves)
            both = mm(sq[s], w)
            f = both[:, 128:]
            r = lax.rsqrt(both[:, :128])
            kernels.append((f * r * (r * r)).astype(bf16))
            values.append(dens[s])
        near[l] = mm(jnp.concatenate(values, 1), jnp.concatenate(kernels, 0))
        return c

    cuts = (0, 24, 64, leaves)
    unroll = 2
    lax.fori_loop(cuts[0], cuts[1], near_leaf, 0, unroll=unroll)

    def wait_terms(k, c):
        other = lax.rem(gy + k, ny)
        pltpu.make_async_remote_copy(
            src_ref=term_all.at[other], dst_ref=term_all.at[other], send_sem=term_send.at[k],
            recv_sem=term_recv.at[other], device_id=(gx, other), device_id_type=MESH,
        ).wait_recv()
        return c

    lax.fori_loop(1, ny, wait_terms, 0)
    total = term_all[0]
    for u in range(1, ny):
        total = total + term_all[u]
    top_all[gx] = total.astype(bf16)

    def start_tops(k, c):
        top_copy(k).start()
        return c

    lax.fori_loop(1, nx, start_tops, 0)
    for side in range(2):
        coeff_copy(side).start()
    own_coeff = pltpu.make_async_copy(coeff, coeff_out.at[1], out_sem.at[0])
    own_coeff.start()
    lift_copy = pltpu.make_async_copy(lift, lift_out, out_sem.at[1])
    lift_copy.start()
    halo_copy = pltpu.make_async_copy(dens.at[pl.ds(leaves, 2 * HALO)], dens_halo_out, out_sem.at[2])
    halo_copy.start()
    geo_copy = pltpu.make_async_copy(geo_halo, geo_halo_out, out_sem.at[3])
    geo_copy.start()

    lax.fori_loop(cuts[1], cuts[2], near_leaf, 0, unroll=unroll)
    near_copies = [
        pltpu.make_async_copy(near.at[pl.ds(0, cuts[2])], near_out.at[pl.ds(0, cuts[2])], out_sem.at[4]),
        pltpu.make_async_copy(
            near.at[pl.ds(cuts[2], leaves - cuts[2])], near_out.at[pl.ds(cuts[2], leaves - cuts[2])], out_sem.at[5]
        ),
    ]
    near_copies[0].start()

    def wait_tops(k, c):
        other = lax.rem(gx + k, nx)
        pltpu.make_async_remote_copy(
            src_ref=top_all.at[other], dst_ref=top_all.at[other], send_sem=top_send.at[k],
            recv_sem=top_recv.at[other], device_id=(other, gy), device_id_type=MESH,
        ).wait_recv()
        return c

    def wait_mid(slot, k):
        pltpu.make_async_remote_copy(
            src_ref=mid_all.at[slot], dst_ref=mid_all.at[slot], send_sem=mid_send.at[0, k],
            recv_sem=mid_recv.at[slot], device_id=(gx, lax.rem(gy + 1, ny)), device_id_type=MESH,
        ).wait_recv()

    def wait_mids(k, c):
        other = lax.rem(gy + k, ny)
        for g in range(3):
            wait_mid(g * ny + other, k)
        return c

    lax.fori_loop(1, nx, wait_tops, 0)
    wait_mid(gy, 0)
    wait_mid(2 * ny + gy, 0)
    lax.fori_loop(1, ny, wait_mids, 0)
    loads[2].wait()

    root_field = jnp.zeros((32, 64), f32)
    for q in range(nx // BRANCH):
        root = jnp.zeros((32, 64), f32)
        for j in range(BRANCH):
            g = q * BRANCH + j
            root = root + nt(unfold(top_all[g]), group_up[g])
        root_field = root_field + nt(root.astype(bf16), root_row[q])
    top_field = nt(root_field.astype(bf16), group_down[0])
    for f in range(group_coupling.shape[1]):
        top_field = top_field + nt(unfold(top_all[group_far[0, f]]), group_coupling[0, f])
    mid_field = nt(top_field.astype(bf16), cluster_down[0])
    for f in range(cluster_coupling.shape[1]):
        u = jnp.clip(cluster_far[0, f] - (gx - 1) * ny, 0, 3 * ny - 1)
        mid_field = mid_field + nt(unfold(mid_all[u]), cluster_coupling[0, f])
    mid_out[...] = jnp.concatenate([mid_field, jnp.zeros((32, 64), f32)], axis=1).astype(bf16)

    lax.fori_loop(cuts[2], leaves, near_leaf, 0, unroll=unroll)
    near_copies[1].start()

    def finish_y(k, c):
        term_copy(k).wait_send()
        for g in range(3):
            mid_copy(g, k).wait_send()
        return c

    def finish_x(k, c):
        top_copy(k).wait_send()
        return c

    lax.fori_loop(1, ny, finish_y, 0)
    mid_copy(0, 0).wait_send()
    mid_copy(2, 0).wait_send()
    lax.fori_loop(1, nx, finish_x, 0)
    for side in range(2):
        coeff_copy(side).wait()
    for c in (own_coeff, lift_copy, halo_copy, geo_copy, *near_copies):
        c.wait()


def down_kernel(
    leaves, first_ref, extent, far, count, near_ids, mid, coupling_hbm, lift_hbm, coeff_hbm, near_hbm, basis_hbm,
    geo_hbm, geo_halo_hbm, dens_hbm, dens_halo_hbm,
    out_hbm,
    coupling, lift, pair, dup, near, basis, relay, out, geo, geo_halo, dens, in_sem, out_sem, slow_sem,
):
    first = first_ref[0]
    chunks = 8
    step = 64 // chunks
    pieces = [
        pltpu.make_async_copy(
            coupling_hbm.at[:, pl.ds(k * step, step)], coupling.at[:, pl.ds(k * step, step)], in_sem.at[k]
        )
        for k in range(chunks)
    ]
    coeff_in = pltpu.make_async_copy(coeff_hbm, pair, in_sem.at[chunks])
    others = [
        pltpu.make_async_copy(lift_hbm, lift, in_sem.at[chunks + 1]),
        pltpu.make_async_copy(basis_hbm, basis, in_sem.at[chunks + 2]),
        pltpu.make_async_copy(near_hbm, near, in_sem.at[chunks + 3]),
    ]
    for c in pieces[:4]:
        c.start()
    coeff_in.start()
    for c in pieces[4:]:
        c.start()
    for c in others:
        c.start()

    ident = eye(leaves)
    for k in range(chunks):
        pieces[k].wait()

        def relayout(h, c):
            i = 2 * h
            for f in range(3):
                x = jnp.concatenate(
                    [coupling[2 * f, i], coupling[2 * f + 1, i], coupling[2 * f, i + 1], coupling[2 * f + 1, i + 1]], 0
                )
                y = nt(ident, x)
                relay[f, pl.ds(i * RPITCH, leaves), :] = y[:, :128]
                relay[f, pl.ds((i + 1) * RPITCH, leaves), :] = y[:, 128:]
            return c

        lax.fori_loop(k * step // 2, (k + 1) * step // 2, relayout, 0, unroll=2)

    coeff_in.wait()
    low = low_lanes((32, 128))

    def spread(p, c):
        for side in range(3):
            tile = pair[side, p].astype(f32)
            turned = pltpu.roll(tile, 64, 1)
            dup[side * leaves + 2 * p] = jnp.where(low, tile, turned).astype(bf16)
            dup[side * leaves + 2 * p + 1] = jnp.where(low, turned, tile).astype(bf16)
        return c

    lax.fori_loop(0, leaves // 2, spread, 0, unroll=2)
    dup[3 * leaves] = jnp.zeros((32, 128), bf16)
    for c in others:
        c.wait()

    @pl.when(jnp.logical_not(jnp.max(extent[...]) < FAR_LIMIT))
    def _():
        copies = [
            pltpu.make_async_copy(geo_hbm, geo, slow_sem.at[0]),
            pltpu.make_async_copy(geo_halo_hbm, geo_halo, slow_sem.at[1]),
            pltpu.make_async_copy(dens_hbm, dens.at[pl.ds(0, leaves)], slow_sem.at[2]),
            pltpu.make_async_copy(dens_halo_hbm, dens.at[pl.ds(leaves, 2 * HALO)], slow_sem.at[3]),
        ]
        for c in copies:
            c.start()
        for c in copies:
            c.wait()

        def leaf(l, c):
            near[l] = jnp.zeros((32, 128), f32)

            def one(n, c):
                s = slot_of(near_ids[n, l], first, leaves)
                rows = []
                for k in range(7):
                    local = geo[k, pl.ds(jnp.minimum(s, leaves - 1), 1), :]
                    sl = geo_halo[0, k, pl.ds(jnp.clip(s - leaves, 0, HALO - 1), 1), :]
                    sr = geo_halo[1, k, pl.ds(jnp.clip(s - leaves - HALO, 0, HALO - 1), 1), :]
                    rows.append(jnp.where(s < leaves, local, jnp.where(s < leaves + HALO, sl, sr)))
                rows.append(jnp.zeros((1, 128), f32))
                cols = jnp.concatenate(rows, axis=0).T
                off = [geo[k, pl.ds(l, 1), :] - cols[:, k : k + 1] for k in range(3)]
                area = cols[:, 6:7]
                spread_ = off[0] * off[0] + off[1] * off[1] + off[2] * off[2] + area
                facing = cols[:, 3:4] * off[0] + cols[:, 4:5] * off[1] + cols[:, 5:6] * off[2]
                kern = area * facing / (4.0 * math.pi * spread_ * jnp.sqrt(spread_))
                near[l] += mm(dens[s], kern.astype(bf16))
                return c

            return lax.fori_loop(0, 8, one, c)

        lax.fori_loop(0, leaves, leaf, 0)

    parent = mid[...]

    def leaf(l, c):
        lhs, mats = [], []
        for f in range(3):
            tiles = []
            for b in range(2):
                k = 2 * f + b
                s = jnp.where(k < count[l], far[k, l] - (first - leaves), 3 * leaves)
                s = jnp.clip(s, 0, 3 * leaves)
                tiles.append(dup[s])
            lhs.append(jnp.where(low, tiles[0], tiles[1]))
            mats.append(relay[f, pl.ds(l, 64, RPITCH), :].astype(bf16))
        lhs.append(parent)
        mats.append(lift[l])
        field = nt(jnp.concatenate(lhs, 1), jnp.concatenate(mats, 1)).astype(bf16)
        out[l] = mm(field, basis[l]) + near[l]
        return c

    parts = 4
    size = leaves // parts
    stores = []
    for k in range(parts):
        lax.fori_loop(k * size, (k + 1) * size, leaf, 0, unroll=4)
        stores.append(
            pltpu.make_async_copy(out.at[pl.ds(k * size, size)], out_hbm.at[pl.ds(k * size, size)], out_sem.at[k])
        )
        stores[-1].start()
    for c in stores:
        c.wait()


def on_device(
    nx, ny, densities, geometry, near_ids, basis_in, basis_out, leaf_up, leaf_down, leaf_coupling, leaf_far, leaf_count,
    cluster_up, cluster_down, cluster_coupling, cluster_far, group_up, group_down, group_coupling, group_far,
    root_coupling,
):
    leaves = densities.shape[0]
    slots = leaves + 2 * HALO
    geo = jnp.transpose(geometry, (1, 0, 2))
    up = jnp.transpose(leaf_up, (1, 2, 0))
    down = jnp.transpose(leaf_down, (1, 2, 0))
    coupling = jnp.transpose(leaf_coupling, (1, 2, 3, 0))
    ids = near_ids.T
    far = leaf_far.T
    V = pl.BlockSpec(memory_space=pltpu.VMEM)
    S = pl.BlockSpec(memory_space=pltpu.SMEM)
    H = pl.BlockSpec(memory_space=pl.ANY)
    dma = pltpu.SemaphoreType.DMA
    shape = jax.ShapeDtypeStruct
    near, lift, coeff, mid, extent, dens_halo, geo_halo = pl.pallas_call(
        functools.partial(up_kernel, nx, ny, leaves),
        name="up",
        out_shape=(
            shape((leaves, 32, 128), f32),
            shape((leaves, 64, 128), bf16),
            shape((3, leaves // 2, 32, 128), bf16),
            shape((32, 128), bf16),
            shape((8, 128), f32),
            shape((2 * HALO, 32, 128), bf16),
            shape((2, 7, HALO, 128), f32),
        ),
        in_specs=[V, S, S, S, H, H, V, V, V, V, V, V, V, V, H],
        out_specs=(H, H, H, V, V, H, H),
        scratch_shapes=[
            pltpu.VMEM((slots, 32, 128), bf16),
            pltpu.VMEM((leaves, 64, 128), bf16),
            pltpu.VMEM((2, 7, HALO, 128), f32),
            pltpu.VMEM((slots * SPITCH, 128), f32),
            pltpu.VMEM((leaves * TPITCH, 128), f32),
            pltpu.VMEM((slots, 128, 64), bf16),
            pltpu.VMEM((64 * RPITCH, 128), f32),
            pltpu.VMEM((leaves, 64, 128), bf16),
            pltpu.VMEM((leaves // 2, 32, 128), bf16),
            pltpu.VMEM((3 * ny, 16, 128), bf16),
            pltpu.VMEM((ny, 16, 128), f32),
            pltpu.VMEM((nx, 16, 128), bf16),
            pltpu.VMEM((nx // BRANCH, 64, 64), bf16),
            pltpu.VMEM((leaves, 32, 128), f32),
            dma((3,)), dma((6,)), dma((4,)), dma((4,)), dma((2,)), dma((2,)), dma((3, ny)), dma((3 * ny,)),
            dma((ny,)), dma((ny,)), dma((nx,)), dma((nx,)),
        ],
        compiler_params=pltpu.CompilerParams(
            collective_id=0, has_side_effects=True, vmem_limit_bytes=48 << 20
        ),
    )(
        geo, ids, cluster_far, group_far, densities, basis_in, up, down, cluster_up, cluster_down, cluster_coupling,
        group_up, group_down, group_coupling, root_coupling,
    )
    first = ((lax.axis_index("gx") * ny + lax.axis_index("gy")) * leaves).reshape(1)
    return pl.pallas_call(
        functools.partial(down_kernel, leaves),
        name="down",
        out_shape=shape((leaves, 32, 128), f32),
        in_specs=[S, V, S, S, S, V] + [H] * 9,
        out_specs=H,
        scratch_shapes=[
            pltpu.VMEM((6, 64, 64, leaves), bf16),
            pltpu.VMEM((leaves, 64, 128), bf16),
            pltpu.VMEM((3, leaves // 2, 32, 128), bf16),
            pltpu.VMEM((3 * leaves + 1, 32, 128), bf16),
            pltpu.VMEM((leaves, 32, 128), f32),
            pltpu.VMEM((leaves, 64, 128), bf16),
            pltpu.VMEM((3, 64 * RPITCH, 128), f32),
            pltpu.VMEM((leaves, 32, 128), f32),
            pltpu.VMEM((7, leaves, 128), f32),
            pltpu.VMEM((2, 7, HALO, 128), f32),
            pltpu.VMEM((slots, 32, 128), bf16),
            dma((12,)), dma((4,)), dma((4,)),
        ],
        compiler_params=pltpu.CompilerParams(vmem_limit_bytes=48 << 20),
    )(
        first, extent, far, leaf_count, ids, mid, coupling, lift, coeff, near, basis_out, geo, geo_halo, densities,
        dens_halo,
    )


def solution(mesh):
    leaf = ("gx", "gy")
    return jax.shard_map(
        functools.partial(on_device, mesh.shape["gx"], mesh.shape["gy"]),
        mesh=mesh,
        in_specs=(
            P(leaf, None, None),
            P(leaf, None, None),
            P(leaf, None),
            P(leaf, None, None),
            P(leaf, None, None),
            P(leaf, None, None),
            P(leaf, None, None),
            P(leaf, None, None, None),
            P(leaf, None),
            P(leaf),
            P(leaf, None, None),
            P(leaf, None, None),
            P(leaf, None, None, None),
            P(leaf, None),
            P(),
            P("gx", None, None),
            P("gx", None, None, None),
            P("gx", None),
            P(),
        ),
        out_specs=P(leaf, None, None),
        check_vma=False,
    )
```

```python
import functools
import math

import jax
import jax.numpy as jnp
from jax import lax
from jax.experimental import pallas as pl
from jax.experimental.pallas import tpu as pltpu
from jax.sharding import PartitionSpec as P

f32 = jnp.float32
bf16 = jnp.bfloat16
MESH = pl.DeviceIdType.MESH
NT = (((1,), (1,)), ((), ()))

REACH = 4
BRANCH = 4
HALO = 8
CHUNK = 8
SPITCH = 65
TPITCH = 33
RPITCH = 97
FAR_LIMIT = 4096.0
VMEM_LIMIT = 67043328


def nt(a, b):
    return lax.dot_general(a, b, NT, preferred_element_type=f32)


def mm(a, b):
    return jnp.dot(a, b, preferred_element_type=f32)


def eye(n):
    rows = lax.broadcasted_iota(jnp.int32, (n, n), 0)
    cols = lax.broadcasted_iota(jnp.int32, (n, n), 1)
    return jnp.where(rows == cols, 1.0, 0.0).astype(bf16)


def split3(x):
    high = x.astype(bf16).astype(f32)
    rest = x - high
    mid = rest.astype(bf16).astype(f32)
    return high, mid, rest - mid


def low_lanes(shape):
    return lax.broadcasted_iota(jnp.int32, shape, len(shape) - 1) < 64


def fold(x):
    return jnp.concatenate([x[:16], x[16:]], axis=1)


def unfold(x):
    return jnp.concatenate([x[:, :64], x[:, 64:]], axis=0)


def slot_of(near_id, first, leaves):
    s = near_id - first
    s = jnp.where(s < 0, s + leaves + HALO, jnp.where(s < leaves, s, s + HALO))
    return jnp.clip(s, 0, leaves + 2 * HALO - 1)


def prepare(geo, rows, base, origin, src, tgt):
    u = [geo[k] - origin[k] for k in range(3)]
    area = geo[6]
    weight = area * (1.0 / (4.0 * math.pi))
    m = [geo[3 + k] * weight for k in range(3)]
    norm = u[0] * u[0] + u[1] * u[1] + u[2] * u[2]
    shift = -(m[0] * u[0] + m[1] * u[1] + m[2] * u[2])
    one = jnp.ones_like(norm)
    zero = jnp.zeros_like(norm)
    us = [split3(x) for x in u]
    vs = [tuple(-2.0 * y for y in x) for x in us]
    ms = [split3(x) for x in m]

    def put(ref, pitch, row, val):
        ref[pl.ds(base * pitch + row, rows, pitch), :] = val

    row = 0
    for k in range(3):
        for i, j in ((0, 0), (0, 1), (1, 0), (0, 2), (2, 0), (1, 1)):
            put(src, SPITCH, row, vs[k][i])
            put(src, SPITCH, 32 + row, ms[k][i])
            if tgt is not None:
                put(tgt, TPITCH, row, us[k][j])
            row += 1
    norms, totals, shifts = split3(norm), split3(norm + area), split3(shift)
    for i in range(3):
        put(src, SPITCH, row, one)
        put(src, SPITCH, 32 + row, zero)
        if tgt is not None:
            put(tgt, TPITCH, row, norms[i])
        row += 1
    for i in range(3):
        put(src, SPITCH, row, totals[i])
        put(src, SPITCH, 32 + row, shifts[i])
        if tgt is not None:
            put(tgt, TPITCH, row, one)
        row += 1
    for r in range(row, 32):
        put(src, SPITCH, r, zero)
        put(src, SPITCH, 32 + r, zero)
        if tgt is not None:
            put(tgt, TPITCH, r, zero)
    return jnp.max(norm)


def up_kernel(
    nx, ny, leaves,
    ids, cluster_far, group_far, geo_hbm, dens_hbm, basis_hbm, up_hbm, down_hbm, cluster_up_hbm, cluster_down_hbm,
    cluster_coupling_hbm, group_up_hbm, group_down_hbm, group_coupling_hbm, root_hbm,
    near_out, lift_out, coeff_out, mid_out, extent_out, dens_halo_out, geo_halo_out,
    geo, dens, basis, up, down, cluster_up, cluster_down, cluster_coupling, group_up, group_down, group_coupling,
    geo_halo, src, tgt, sq, relay, lift, coeff, lhs_all, mid_all, term_all, top_all, root_row, pairs_buf, near,
    in_sem, out_sem, halo_send, halo_recv, coeff_send, coeff_recv, mid_send, mid_recv, term_send, term_recv,
    top_send, top_recv,
):
    gx = lax.axis_index("gx")
    gy = lax.axis_index("gy")
    first = (gx * ny + gy) * leaves
    pairs = leaves // 2
    next_x = lax.rem(gx + 1, nx)
    prev_x = lax.rem(gx + nx - 1, nx)
    right = (jnp.where(gy == ny - 1, next_x, gx), lax.rem(gy + 1, ny))
    left = (jnp.where(gy == 0, prev_x, gx), lax.rem(gy + ny - 1, ny))

    moves = (
        (geo_hbm, geo),
        (down_hbm, down),
        (up_hbm, up),
        (dens_hbm, dens.at[pl.ds(0, leaves)]),
        (basis_hbm, basis),
        (cluster_up_hbm, cluster_up),
        (root_hbm.at[gx // BRANCH], root_row),
        (group_up_hbm, group_up),
        (group_down_hbm, group_down),
        (group_coupling_hbm, group_coupling),
        (cluster_down_hbm, cluster_down),
        (cluster_coupling_hbm, cluster_coupling),
    )
    loads = [pltpu.make_async_copy(a, b, in_sem.at[k]) for k, (a, b) in enumerate(moves)]
    for c in loads:
        c.start()

    barrier = pltpu.get_barrier_semaphore()

    def greet_x(k, c):
        pl.semaphore_signal(barrier, inc=1, device_id=(lax.rem(gx + k, nx), gy), device_id_type=MESH)
        return c

    def greet_y(k, c):
        other = lax.rem(gy + k, ny)
        for x in (prev_x, gx, next_x):
            pl.semaphore_signal(barrier, inc=1, device_id=(x, other), device_id_type=MESH)
        return c

    lax.fori_loop(1, nx, greet_x, 0)
    lax.fori_loop(1, ny, greet_y, 0)

    loads[0].wait()
    origin = [jnp.mean(geo[k, leaves // 2 : leaves // 2 + 1, :], axis=1, keepdims=True) for k in range(3)]
    extent = prepare(geo, leaves, 0, origin, src, tgt)

    ident = eye(leaves)
    loads[1].wait()
    loads[2].wait()

    def relayout(h, c):
        i = 2 * h
        x = jnp.concatenate([down[i], up[i], down[i + 1], up[i + 1]], axis=0)
        y = nt(ident, x)
        relay[pl.ds(i * RPITCH, leaves), :] = y[:, :128]
        relay[pl.ds((i + 1) * RPITCH, leaves), :] = y[:, 128:]
        return c

    lax.fori_loop(0, 32, relayout, 0, unroll=4)

    pl.semaphore_wait(barrier, (nx - 1) + 3 * (ny - 1))
    loads[3].wait()
    halo = []
    for side, (dest, leaf0, row0) in enumerate(
        ((right, leaves - REACH, leaves + HALO - REACH), (left, 0, leaves + HALO))
    ):
        halo.append(
            pltpu.make_async_remote_copy(
                src_ref=dens.at[pl.ds(leaf0, REACH)],
                dst_ref=dens.at[pl.ds(row0, REACH)],
                send_sem=halo_send.at[2 * side],
                recv_sem=halo_recv.at[2 * side],
                device_id=dest,
                device_id_type=MESH,
            )
        )
        halo.append(
            pltpu.make_async_remote_copy(
                src_ref=geo.at[:, pl.ds((leaves - HALO) * (1 - side), HALO), :],
                dst_ref=geo_halo.at[side],
                send_sem=halo_send.at[2 * side + 1],
                recv_sem=halo_recv.at[2 * side + 1],
                device_id=dest,
                device_id_type=MESH,
            )
        )
    for c in halo:
        c.start()

    loads[4].wait()
    low = low_lanes((32, 128))

    def leaf_coeffs(p, c):
        x = dens[pl.ds(2 * p, 2)].reshape(64, 128)
        w = basis[pl.ds(2 * p, 2)].reshape(128, 128)
        y = nt(x, w)
        tile = jnp.where(low, y[:32], y[32:])
        coeff[p] = tile.astype(bf16)
        turned = pltpu.roll(tile, 64, 1)
        lhs_all[p] = jnp.concatenate([jnp.where(low, 0.0, turned), jnp.where(low, 0.0, tile)], axis=1).astype(bf16)
        return c

    def upward(p, acc):
        mats = []
        for b in range(2):
            mat = relay[pl.ds(2 * p + b, 64, RPITCH), :].astype(bf16)
            lift[2 * p + b] = mat
            mats.append(mat)
        return acc + nt(lhs_all[p], jnp.concatenate(mats, axis=1))

    lax.fori_loop(0, pairs, leaf_coeffs, 0, unroll=8)
    mid = lax.fori_loop(0, pairs, upward, jnp.zeros((32, 64), f32), unroll=8)
    loads[5].wait()
    mid = mid.astype(bf16)
    term = nt(mid, cluster_up[0])
    mid_all[ny + gy] = fold(mid.astype(f32)).astype(bf16)
    term_all[gy] = fold(term)

    def term_copy(k):
        other = lax.rem(gy + k, ny)
        return pltpu.make_async_remote_copy(
            src_ref=term_all.at[gy], dst_ref=term_all.at[gy], send_sem=term_send.at[k], recv_sem=term_recv.at[gy],
            device_id=(gx, other), device_id_type=MESH,
        )

    def mid_copy(g, k):
        other = lax.rem(gy + k, ny)
        x = (next_x, gx, prev_x)[g]
        return pltpu.make_async_remote_copy(
            src_ref=mid_all.at[ny + gy], dst_ref=mid_all.at[g * ny + gy], send_sem=mid_send.at[g, k],
            recv_sem=mid_recv.at[g * ny + gy], device_id=(x, other), device_id_type=MESH,
        )

    def top_copy(k):
        return pltpu.make_async_remote_copy(
            src_ref=top_all.at[gx], dst_ref=top_all.at[gx], send_sem=top_send.at[k], recv_sem=top_recv.at[gx],
            device_id=(lax.rem(gx + k, nx), gy), device_id_type=MESH,
        )

    def coeff_copy(side):
        dest = (right, left)[side]
        return pltpu.make_async_remote_copy(
            src_ref=coeff, dst_ref=coeff_out.at[2 * side], send_sem=coeff_send.at[side], recv_sem=coeff_recv.at[side],
            device_id=dest, device_id_type=MESH,
        )

    def start_terms(k, c):
        term_copy(k).start()
        return c

    def start_mids(k, c):
        for g in range(3):
            mid_copy(g, k).start()
        return c

    lax.fori_loop(1, ny, start_terms, 0)
    mid_copy(0, 0).start()
    mid_copy(2, 0).start()
    lax.fori_loop(1, ny, start_mids, 0)

    for c in halo:
        c.wait()
    for side in range(2):
        extent = jnp.maximum(
            extent, prepare(geo_halo.at[side], HALO, leaves + HALO * side, origin, src, None)
        )
    extent_out[...] = jnp.full(extent_out.shape, extent, f32)

    turn = eye(128)

    def transpose(s, c):
        x = src[pl.ds(s * SPITCH, 64), :].astype(bf16)
        sq[s] = nt(turn, x).astype(bf16)
        return c

    lax.fori_loop(0, leaves + 2 * HALO, transpose, 0, unroll=8)
    zero = jnp.zeros((32, 128), bf16)

    def near_chunk(k, c):
        def kernels(b, c):
            l = k * CHUNK + b
            t = tgt[pl.ds(l * TPITCH, 32), :].astype(bf16)
            w = jnp.concatenate([jnp.concatenate([t, zero], 1), jnp.concatenate([zero, t], 1)], 0)
            for n in range(8):
                both = mm(sq[slot_of(ids[n, l], first, leaves)], w)
                f = both[:, 128:]
                r = lax.rsqrt(both[:, :128])
                pairs_buf[b, pl.ds(n * 128, 128), :] = (f * r * (r * r)).astype(bf16)
            return c

        def apply(b, c):
            l = k * CHUNK + b
            values = [dens[slot_of(ids[n, l], first, leaves)] for n in range(8)]
            near[l] = mm(jnp.concatenate(values, 1), pairs_buf[b])
            return c

        lax.fori_loop(0, CHUNK, kernels, 0, unroll=4)
        lax.fori_loop(0, CHUNK, apply, 0, unroll=4)
        return c

    cuts = (0, 3 * CHUNK, 8 * CHUNK, leaves)

    def near_range(a, b):
        lax.fori_loop(a // CHUNK, b // CHUNK, near_chunk, 0)

    near_range(cuts[0], cuts[1])

    def wait_terms(k, c):
        other = lax.rem(gy + k, ny)
        pltpu.make_async_remote_copy(
            src_ref=term_all.at[other], dst_ref=term_all.at[other], send_sem=term_send.at[k],
            recv_sem=term_recv.at[other], device_id=(gx, other), device_id_type=MESH,
        ).wait_recv()
        return c

    lax.fori_loop(1, ny, wait_terms, 0)
    total = term_all[0]
    for u in range(1, ny):
        total = total + term_all[u]
    top_all[gx] = total.astype(bf16)

    def start_tops(k, c):
        top_copy(k).start()
        return c

    lax.fori_loop(1, nx, start_tops, 0)
    for side in range(2):
        coeff_copy(side).start()
    own_coeff = pltpu.make_async_copy(coeff, coeff_out.at[1], out_sem.at[0])
    own_coeff.start()
    lift_copy = pltpu.make_async_copy(lift, lift_out, out_sem.at[1])
    lift_copy.start()
    halo_copy = pltpu.make_async_copy(dens.at[pl.ds(leaves, 2 * HALO)], dens_halo_out, out_sem.at[2])
    halo_copy.start()
    geo_copy = pltpu.make_async_copy(geo_halo, geo_halo_out, out_sem.at[3])
    geo_copy.start()

    near_range(cuts[1], cuts[2])
    near_copies = [
        pltpu.make_async_copy(near.at[pl.ds(0, cuts[2])], near_out.at[pl.ds(0, cuts[2])], out_sem.at[4]),
        pltpu.make_async_copy(
            near.at[pl.ds(cuts[2], leaves - cuts[2])], near_out.at[pl.ds(cuts[2], leaves - cuts[2])], out_sem.at[5]
        ),
    ]
    near_copies[0].start()

    def wait_tops(k, c):
        other = lax.rem(gx + k, nx)
        pltpu.make_async_remote_copy(
            src_ref=top_all.at[other], dst_ref=top_all.at[other], send_sem=top_send.at[k],
            recv_sem=top_recv.at[other], device_id=(other, gy), device_id_type=MESH,
        ).wait_recv()
        return c

    def wait_mid(slot, k):
        pltpu.make_async_remote_copy(
            src_ref=mid_all.at[slot], dst_ref=mid_all.at[slot], send_sem=mid_send.at[0, k],
            recv_sem=mid_recv.at[slot], device_id=(gx, lax.rem(gy + 1, ny)), device_id_type=MESH,
        ).wait_recv()

    def wait_mids(k, c):
        other = lax.rem(gy + k, ny)
        for g in range(3):
            wait_mid(g * ny + other, k)
        return c

    lax.fori_loop(1, nx, wait_tops, 0)
    wait_mid(gy, 0)
    wait_mid(2 * ny + gy, 0)
    lax.fori_loop(1, ny, wait_mids, 0)
    for c in loads[6:]:
        c.wait()

    root_field = jnp.zeros((32, 64), f32)
    for q in range(nx // BRANCH):
        root = jnp.zeros((32, 64), f32)
        for j in range(BRANCH):
            g = q * BRANCH + j
            root = root + nt(unfold(top_all[g]), group_up[g])
        root_field = root_field + nt(root.astype(bf16), root_row[q])
    top_field = nt(root_field.astype(bf16), group_down[0])
    for f in range(group_coupling.shape[1]):
        top_field = top_field + nt(unfold(top_all[group_far[0, f]]), group_coupling[0, f])
    mid_field = nt(top_field.astype(bf16), cluster_down[0])
    for f in range(cluster_coupling.shape[1]):
        u = jnp.clip(cluster_far[0, f] - (gx - 1) * ny, 0, 3 * ny - 1)
        mid_field = mid_field + nt(unfold(mid_all[u]), cluster_coupling[0, f])
    mid_out[...] = jnp.concatenate([mid_field, jnp.zeros((32, 64), f32)], axis=1).astype(bf16)

    near_range(cuts[2], leaves)
    near_copies[1].start()

    def finish_y(k, c):
        term_copy(k).wait_send()
        for g in range(3):
            mid_copy(g, k).wait_send()
        return c

    def finish_x(k, c):
        top_copy(k).wait_send()
        return c

    lax.fori_loop(1, ny, finish_y, 0)
    mid_copy(0, 0).wait_send()
    mid_copy(2, 0).wait_send()
    lax.fori_loop(1, nx, finish_x, 0)
    for side in range(2):
        coeff_copy(side).wait()
    for c in (own_coeff, lift_copy, halo_copy, geo_copy, *near_copies):
        c.wait()


def down_kernel(
    leaves, first_ref, extent, far, count, near_ids, mid, coupling_hbm, lift_hbm, coeff_hbm, near_hbm, basis_hbm,
    geo_hbm, geo_halo_hbm, dens_hbm, dens_halo_hbm,
    out_hbm,
    coupling, lift, pair, dup, near, basis, relay, fields, out, geo, geo_halo, dens, in_sem, out_sem, slow_sem,
):
    first = first_ref[0]
    chunks = 8
    step = 64 // chunks
    pieces = [
        pltpu.make_async_copy(
            coupling_hbm.at[:, pl.ds(k * step, step)], coupling.at[:, pl.ds(k * step, step)], in_sem.at[k]
        )
        for k in range(chunks)
    ]
    coeff_in = pltpu.make_async_copy(coeff_hbm, pair, in_sem.at[chunks])
    others = [
        pltpu.make_async_copy(lift_hbm, lift, in_sem.at[chunks + 1]),
        pltpu.make_async_copy(basis_hbm, basis, in_sem.at[chunks + 2]),
        pltpu.make_async_copy(near_hbm, near, in_sem.at[chunks + 3]),
    ]
    for c in pieces[:4]:
        c.start()
    coeff_in.start()
    for c in pieces[4:]:
        c.start()
    for c in others:
        c.start()

    ident = eye(leaves)
    for k in range(chunks):
        pieces[k].wait()

        def relayout(h, c):
            i = 2 * h
            for f in range(3):
                x = jnp.concatenate(
                    [coupling[2 * f, i], coupling[2 * f + 1, i], coupling[2 * f, i + 1], coupling[2 * f + 1, i + 1]], 0
                )
                y = nt(ident, x)
                relay[f, pl.ds(i * RPITCH, leaves), :] = y[:, :128]
                relay[f, pl.ds((i + 1) * RPITCH, leaves), :] = y[:, 128:]
            return c

        lax.fori_loop(k * step // 2, (k + 1) * step // 2, relayout, 0, unroll=2)

    coeff_in.wait()
    low = low_lanes((32, 128))

    def spread(p, c):
        for side in range(3):
            tile = pair[side, p].astype(f32)
            turned = pltpu.roll(tile, 64, 1)
            dup[side * leaves + 2 * p] = jnp.where(low, tile, turned).astype(bf16)
            dup[side * leaves + 2 * p + 1] = jnp.where(low, turned, tile).astype(bf16)
        return c

    lax.fori_loop(0, leaves // 2, spread, 0, unroll=2)
    dup[3 * leaves] = jnp.zeros((32, 128), bf16)
    for c in others:
        c.wait()

    @pl.when(jnp.logical_not(jnp.max(extent[...]) < FAR_LIMIT))
    def _():
        copies = [
            pltpu.make_async_copy(geo_hbm, geo, slow_sem.at[0]),
            pltpu.make_async_copy(geo_halo_hbm, geo_halo, slow_sem.at[1]),
            pltpu.make_async_copy(dens_hbm, dens.at[pl.ds(0, leaves)], slow_sem.at[2]),
            pltpu.make_async_copy(dens_halo_hbm, dens.at[pl.ds(leaves, 2 * HALO)], slow_sem.at[3]),
        ]
        for c in copies:
            c.start()
        for c in copies:
            c.wait()

        def leaf(l, c):
            near[l] = jnp.zeros((32, 128), f32)

            def one(n, c):
                s = slot_of(near_ids[n, l], first, leaves)
                rows = []
                for k in range(7):
                    local = geo[k, pl.ds(jnp.minimum(s, leaves - 1), 1), :]
                    sl = geo_halo[0, k, pl.ds(jnp.clip(s - leaves, 0, HALO - 1), 1), :]
                    sr = geo_halo[1, k, pl.ds(jnp.clip(s - leaves - HALO, 0, HALO - 1), 1), :]
                    rows.append(jnp.where(s < leaves, local, jnp.where(s < leaves + HALO, sl, sr)))
                rows.append(jnp.zeros((1, 128), f32))
                cols = jnp.concatenate(rows, axis=0).T
                off = [geo[k, pl.ds(l, 1), :] - cols[:, k : k + 1] for k in range(3)]
                area = cols[:, 6:7]
                spread_ = off[0] * off[0] + off[1] * off[1] + off[2] * off[2] + area
                facing = cols[:, 3:4] * off[0] + cols[:, 4:5] * off[1] + cols[:, 5:6] * off[2]
                kern = area * facing / (4.0 * math.pi * spread_ * jnp.sqrt(spread_))
                near[l] += mm(dens[s], kern.astype(bf16))
                return c

            return lax.fori_loop(0, 8, one, c)

        lax.fori_loop(0, leaves, leaf, 0)

    parent = mid[...]

    def leaf(l, c):
        lhs, mats = [], []
        for f in range(3):
            tiles = []
            for b in range(2):
                k = 2 * f + b
                s = jnp.where(k < count[l], far[k, l] - (first - leaves), 3 * leaves)
                s = jnp.clip(s, 0, 3 * leaves)
                tiles.append(dup[s])
            lhs.append(jnp.where(low, tiles[0], tiles[1]))
            mats.append(relay[f, pl.ds(l, 64, RPITCH), :].astype(bf16))
        lhs.append(parent)
        mats.append(lift[l])
        fields[l] = nt(jnp.concatenate(lhs, 1), jnp.concatenate(mats, 1)).astype(bf16)
        return c

    def panels(l, c):
        out[l] = mm(fields[l], basis[l]) + near[l]
        return c

    parts = 4
    size = leaves // parts
    stores = []
    for k in range(parts):
        lax.fori_loop(k * size, (k + 1) * size, leaf, 0, unroll=8)
        lax.fori_loop(k * size, (k + 1) * size, panels, 0, unroll=8)
        stores.append(
            pltpu.make_async_copy(out.at[pl.ds(k * size, size)], out_hbm.at[pl.ds(k * size, size)], out_sem.at[k])
        )
        stores[-1].start()
    for c in stores:
        c.wait()


def down_call(leaves, *args):
    V = pl.BlockSpec(memory_space=pltpu.VMEM)
    S = pl.BlockSpec(memory_space=pltpu.SMEM)
    H = pl.BlockSpec(memory_space=pl.ANY)
    dma = pltpu.SemaphoreType.DMA
    shape = jax.ShapeDtypeStruct
    slots = leaves + 2 * HALO
    return pl.pallas_call(
        functools.partial(down_kernel, leaves),
        name="down",
        out_shape=shape((leaves, 32, 128), f32),
        in_specs=[S, V, S, S, S, V] + [H] * 9,
        out_specs=H,
        scratch_shapes=[
            pltpu.VMEM((6, 64, 64, leaves), bf16),
            pltpu.VMEM((leaves, 64, 128), bf16),
            pltpu.VMEM((3, leaves // 2, 32, 128), bf16),
            pltpu.VMEM((3 * leaves + 1, 32, 128), bf16),
            pltpu.VMEM((leaves, 32, 128), f32),
            pltpu.VMEM((leaves, 64, 128), bf16),
            pltpu.VMEM((3, 64 * RPITCH, 128), f32),
            pltpu.VMEM((leaves, 32, 64), bf16),
            pltpu.VMEM((leaves, 32, 128), f32),
            pltpu.VMEM((7, leaves, 128), f32),
            pltpu.VMEM((2, 7, HALO, 128), f32),
            pltpu.VMEM((slots, 32, 128), bf16),
            dma((12,)), dma((4,)), dma((4,)),
        ],
        compiler_params=pltpu.CompilerParams(vmem_limit_bytes=VMEM_LIMIT),
    )(*args)


def on_device(
    nx, ny, densities, geometry, near_ids, basis_in, basis_out, leaf_up, leaf_down, leaf_coupling, leaf_far, leaf_count,
    cluster_up, cluster_down, cluster_coupling, cluster_far, group_up, group_down, group_coupling, group_far,
    root_coupling,
):
    leaves = densities.shape[0]
    slots = leaves + 2 * HALO
    geo = jnp.transpose(geometry, (1, 0, 2))
    up = jnp.transpose(leaf_up, (1, 2, 0))
    down = jnp.transpose(leaf_down, (1, 2, 0))
    coupling = jnp.transpose(leaf_coupling, (1, 2, 3, 0))
    ids = near_ids.T
    far = leaf_far.T
    V = pl.BlockSpec(memory_space=pltpu.VMEM)
    S = pl.BlockSpec(memory_space=pltpu.SMEM)
    H = pl.BlockSpec(memory_space=pl.ANY)
    dma = pltpu.SemaphoreType.DMA
    shape = jax.ShapeDtypeStruct
    near, lift, coeff, mid, extent, dens_halo, geo_halo = pl.pallas_call(
        functools.partial(up_kernel, nx, ny, leaves),
        name="up",
        out_shape=(
            shape((leaves, 32, 128), f32),
            shape((leaves, 64, 128), bf16),
            shape((3, leaves // 2, 32, 128), bf16),
            shape((32, 128), bf16),
            shape((8, 128), f32),
            shape((2 * HALO, 32, 128), bf16),
            shape((2, 7, HALO, 128), f32),
        ),
        in_specs=[S, S, S] + [H] * 12,
        out_specs=(H, H, H, V, V, H, H),
        scratch_shapes=[
            pltpu.VMEM((7, leaves, 128), f32),
            pltpu.VMEM((slots, 32, 128), bf16),
            pltpu.VMEM((leaves, 64, 128), bf16),
            pltpu.VMEM((64, 64, leaves), bf16),
            pltpu.VMEM((64, 64, leaves), bf16),
            pltpu.VMEM((1, 64, 64), bf16),
            pltpu.VMEM((1, 64, 64), bf16),
            pltpu.VMEM(cluster_coupling.shape, bf16),
            pltpu.VMEM(group_up.shape, bf16),
            pltpu.VMEM((1, 64, 64), bf16),
            pltpu.VMEM(group_coupling.shape, bf16),
            pltpu.VMEM((2, 7, HALO, 128), f32),
            pltpu.VMEM((slots * SPITCH, 128), f32),
            pltpu.VMEM((leaves * TPITCH, 128), f32),
            pltpu.VMEM((slots, 128, 64), bf16),
            pltpu.VMEM((64 * RPITCH, 128), f32),
            pltpu.VMEM((leaves, 64, 128), bf16),
            pltpu.VMEM((leaves // 2, 32, 128), bf16),
            pltpu.VMEM((leaves // 2, 32, 256), bf16),
            pltpu.VMEM((3 * ny, 16, 128), bf16),
            pltpu.VMEM((ny, 16, 128), f32),
            pltpu.VMEM((nx, 16, 128), bf16),
            pltpu.VMEM((nx // BRANCH, 64, 64), bf16),
            pltpu.VMEM((CHUNK, 8 * 128, 128), bf16),
            pltpu.VMEM((leaves, 32, 128), f32),
            dma((12,)), dma((6,)), dma((4,)), dma((4,)), dma((2,)), dma((2,)), dma((3, ny)), dma((3 * ny,)),
            dma((ny,)), dma((ny,)), dma((nx,)), dma((nx,)),
        ],
        compiler_params=pltpu.CompilerParams(
            collective_id=0, has_side_effects=True, vmem_limit_bytes=VMEM_LIMIT
        ),
    )(
        ids, cluster_far, group_far, geo, densities, basis_in, up, down, cluster_up, cluster_down, cluster_coupling,
        group_up, group_down, group_coupling, root_coupling,
    )
    first = ((lax.axis_index("gx") * ny + lax.axis_index("gy")) * leaves).reshape(1)
    return down_call(
        leaves, first, extent, far, leaf_count, ids, mid, coupling, lift, coeff, near, basis_out, geo, geo_halo,
        densities, dens_halo,
    )


def solution(mesh):
    leaf = ("gx", "gy")
    return jax.shard_map(
        functools.partial(on_device, mesh.shape["gx"], mesh.shape["gy"]),
        mesh=mesh,
        in_specs=(
            P(leaf, None, None),
            P(leaf, None, None),
            P(leaf, None),
            P(leaf, None, None),
            P(leaf, None, None),
            P(leaf, None, None),
            P(leaf, None, None),
            P(leaf, None, None, None),
            P(leaf, None),
            P(leaf),
            P(leaf, None, None),
            P(leaf, None, None),
            P(leaf, None, None, None),
            P(leaf, None),
            P(),
            P("gx", None, None),
            P("gx", None, None, None),
            P("gx", None),
            P(),
        ),
        out_specs=P(leaf, None, None),
        check_vma=False,
    )
```

```python
import functools
import math

import jax
import jax.numpy as jnp
from jax import lax
from jax.experimental import pallas as pl
from jax.experimental.pallas import tpu as pltpu
from jax.sharding import PartitionSpec as P

f32 = jnp.float32
bf16 = jnp.bfloat16
MESH = pl.DeviceIdType.MESH
NT = (((1,), (1,)), ((), ()))

REACH = 4
BRANCH = 4
HALO = 8
CHUNK = 8
SPITCH = 65
TPITCH = 33
RPITCH = 97
FAR_LIMIT = 4096.0
VMEM_LIMIT = 67043328


def nt(a, b):
    return lax.dot_general(a, b, NT, preferred_element_type=f32)


def mm(a, b):
    return jnp.dot(a, b, preferred_element_type=f32)


def eye(n):
    rows = lax.broadcasted_iota(jnp.int32, (n, n), 0)
    cols = lax.broadcasted_iota(jnp.int32, (n, n), 1)
    return jnp.where(rows == cols, 1.0, 0.0).astype(bf16)


def split3(x):
    high = x.astype(bf16).astype(f32)
    rest = x - high
    mid = rest.astype(bf16).astype(f32)
    return high, mid, rest - mid


def low_lanes(shape):
    return lax.broadcasted_iota(jnp.int32, shape, len(shape) - 1) < 64


def fold(x):
    return jnp.concatenate([x[:16], x[16:]], axis=1)


def unfold(x):
    return jnp.concatenate([x[:, :64], x[:, 64:]], axis=0)


def slot_of(near_id, first, leaves):
    s = near_id - first
    s = jnp.where(s < 0, s + leaves + HALO, jnp.where(s < leaves, s, s + HALO))
    return jnp.clip(s, 0, leaves + 2 * HALO - 1)


def prepare(geo, rows, base, origin, src, tgt):
    u = [geo[k] - origin[k] for k in range(3)]
    area = geo[6]
    weight = area * (1.0 / (4.0 * math.pi))
    m = [geo[3 + k] * weight for k in range(3)]
    norm = u[0] * u[0] + u[1] * u[1] + u[2] * u[2]
    shift = -(m[0] * u[0] + m[1] * u[1] + m[2] * u[2])
    one = jnp.ones_like(norm)
    zero = jnp.zeros_like(norm)
    us = [split3(x) for x in u]
    vs = [tuple(-2.0 * y for y in x) for x in us]
    ms = [split3(x) for x in m]

    def put(ref, pitch, row, val):
        ref[pl.ds(base * pitch + row, rows, pitch), :] = val

    row = 0
    for k in range(3):
        for i, j in ((0, 0), (0, 1), (1, 0), (0, 2), (2, 0), (1, 1)):
            put(src, SPITCH, row, vs[k][i])
            put(src, SPITCH, 32 + row, ms[k][i])
            if tgt is not None:
                put(tgt, TPITCH, row, us[k][j])
            row += 1
    norms, totals, shifts = split3(norm), split3(norm + area), split3(shift)
    for i in range(3):
        put(src, SPITCH, row, one)
        put(src, SPITCH, 32 + row, zero)
        if tgt is not None:
            put(tgt, TPITCH, row, norms[i])
        row += 1
    for i in range(3):
        put(src, SPITCH, row, totals[i])
        put(src, SPITCH, 32 + row, shifts[i])
        if tgt is not None:
            put(tgt, TPITCH, row, one)
        row += 1
    for r in range(row, 32):
        put(src, SPITCH, r, zero)
        put(src, SPITCH, 32 + r, zero)
        if tgt is not None:
            put(tgt, TPITCH, r, zero)
    return jnp.max(norm)


def up_kernel(
    nx, ny, leaves,
    ids, far, count, cluster_far, group_far, geo_hbm, dens_hbm, basis_hbm, up_hbm, down_hbm, cluster_up_hbm, cluster_down_hbm,
    cluster_coupling_hbm, group_up_hbm, group_down_hbm, group_coupling_hbm, root_hbm,
    coupling_hbm, panel_basis_hbm,
    total_out, field_out, extent_out, dens_halo_out, geo_halo_out,
    geo, dens, basis, panel_basis, up, down, cluster_up, cluster_down, cluster_coupling, group_up, group_down, group_coupling,
    geo_halo, dens_halo, src, tgt, sq, relay, coupling, coupling_relay, lift, coeff, dup, field, lhs_all, mid_all, term_all, top_all, root_row, pairs_buf, near,
    in_sem, out_sem, halo_send, halo_recv, coeff_send, coeff_recv, mid_send, mid_recv, term_send, term_recv,
    top_send, top_recv,
):
    gx = lax.axis_index("gx")
    gy = lax.axis_index("gy")
    first = (gx * ny + gy) * leaves
    pairs = leaves // 2
    next_x = lax.rem(gx + 1, nx)
    prev_x = lax.rem(gx + nx - 1, nx)
    right = (jnp.where(gy == ny - 1, next_x, gx), lax.rem(gy + 1, ny))
    left = (jnp.where(gy == 0, prev_x, gx), lax.rem(gy + ny - 1, ny))

    moves = (
        (geo_hbm, geo),
        (down_hbm, down),
        (up_hbm, up),
        (dens_hbm, dens.at[pl.ds(0, leaves)]),
        (basis_hbm, basis),
        (cluster_up_hbm, cluster_up),
        (root_hbm.at[gx // BRANCH], root_row),
        (group_up_hbm, group_up),
        (group_down_hbm, group_down),
        (group_coupling_hbm, group_coupling),
        (cluster_down_hbm, cluster_down),
        (cluster_coupling_hbm, cluster_coupling),
        (coupling_hbm, coupling),
        (panel_basis_hbm, panel_basis),
    )
    loads = [pltpu.make_async_copy(a, b, in_sem.at[k]) for k, (a, b) in enumerate(moves)]
    for c in loads:
        c.start()

    barrier = pltpu.get_barrier_semaphore()

    def greet_x(k, c):
        pl.semaphore_signal(barrier, inc=1, device_id=(lax.rem(gx + k, nx), gy), device_id_type=MESH)
        return c

    def greet_y(k, c):
        other = lax.rem(gy + k, ny)
        for x in (prev_x, gx, next_x):
            pl.semaphore_signal(barrier, inc=1, device_id=(x, other), device_id_type=MESH)
        return c

    lax.fori_loop(1, nx, greet_x, 0)
    lax.fori_loop(1, ny, greet_y, 0)

    loads[0].wait()
    origin = [jnp.mean(geo[k, leaves // 2 : leaves // 2 + 1, :], axis=1, keepdims=True) for k in range(3)]
    extent = prepare(geo, leaves, 0, origin, src, tgt)

    ident = eye(leaves)
    loads[1].wait()
    loads[2].wait()

    def relayout(h, c):
        i = 2 * h
        x = jnp.concatenate([down[i], up[i], down[i + 1], up[i + 1]], axis=0)
        y = nt(ident, x)
        relay[pl.ds(i * RPITCH, leaves), :] = y[:, :128]
        relay[pl.ds((i + 1) * RPITCH, leaves), :] = y[:, 128:]
        return c

    lax.fori_loop(0, 32, relayout, 0, unroll=8)

    loads[3].wait()
    loads[4].wait()
    low = low_lanes((32, 128))

    def leaf_coeffs(p, c):
        x = dens[pl.ds(2 * p, 2)].reshape(64, 128)
        w = basis[pl.ds(2 * p, 2)].reshape(128, 128)
        y = nt(x, w)
        tile = jnp.where(low, y[:32], y[32:])
        coeff[1, p] = tile.astype(bf16)
        turned = pltpu.roll(tile, 64, 1)
        lhs_all[p] = jnp.concatenate([jnp.where(low, 0.0, turned), jnp.where(low, 0.0, tile)], axis=1).astype(bf16)
        return c

    def upward(p, acc):
        mats = []
        for b in range(2):
            mat = relay[pl.ds(2 * p + b, 64, RPITCH), :].astype(bf16)
            lift[2 * p + b] = mat
            mats.append(mat)
        return acc + nt(lhs_all[p], jnp.concatenate(mats, axis=1))

    lax.fori_loop(0, pairs, leaf_coeffs, 0, unroll=8)
    mid = lax.fori_loop(0, pairs, upward, jnp.zeros((32, 64), f32), unroll=16)
    loads[5].wait()
    mid = mid.astype(bf16)
    term = nt(mid, cluster_up[0])
    mid_all[ny + gy] = fold(mid.astype(f32)).astype(bf16)
    term_all[gy] = fold(term)

    loads[12].wait()

    def relayout_coupling(h, c):
        i = 2 * h
        for f in range(3):
            x = jnp.concatenate(
                [coupling[2 * f, i], coupling[2 * f + 1, i], coupling[2 * f, i + 1], coupling[2 * f + 1, i + 1]], 0
            )
            y = nt(ident, x)
            coupling_relay[f, pl.ds(i * RPITCH, leaves), :] = y[:, :128]
            coupling_relay[f, pl.ds((i + 1) * RPITCH, leaves), :] = y[:, 128:]
        return c

    lax.fori_loop(0, 32, relayout_coupling, 0, unroll=8)

    pl.semaphore_wait(barrier, (nx - 1) + 3 * (ny - 1))
    halo = []
    for side, (dest, leaf0, row0) in enumerate(
        ((right, leaves - REACH, HALO - REACH), (left, 0, HALO))
    ):
        halo.append(
            pltpu.make_async_remote_copy(
                src_ref=dens.at[pl.ds(leaf0, REACH)],
                dst_ref=dens_halo.at[pl.ds(row0, REACH)],
                send_sem=halo_send.at[2 * side],
                recv_sem=halo_recv.at[2 * side],
                device_id=dest,
                device_id_type=MESH,
            )
        )
        halo.append(
            pltpu.make_async_remote_copy(
                src_ref=geo.at[:, pl.ds((leaves - HALO) * (1 - side), HALO), :],
                dst_ref=geo_halo.at[side],
                send_sem=halo_send.at[2 * side + 1],
                recv_sem=halo_recv.at[2 * side + 1],
                device_id=dest,
                device_id_type=MESH,
            )
        )

    def term_copy(k):
        other = lax.rem(gy + k, ny)
        return pltpu.make_async_remote_copy(
            src_ref=term_all.at[gy], dst_ref=term_all.at[gy], send_sem=term_send.at[k], recv_sem=term_recv.at[gy],
            device_id=(gx, other), device_id_type=MESH,
        )

    def mid_copy(g, k):
        other = lax.rem(gy + k, ny)
        x = (next_x, gx, prev_x)[g]
        return pltpu.make_async_remote_copy(
            src_ref=mid_all.at[ny + gy], dst_ref=mid_all.at[g * ny + gy], send_sem=mid_send.at[g, k],
            recv_sem=mid_recv.at[g * ny + gy], device_id=(x, other), device_id_type=MESH,
        )

    def top_copy(k):
        return pltpu.make_async_remote_copy(
            src_ref=top_all.at[gx], dst_ref=top_all.at[gx], send_sem=top_send.at[k], recv_sem=top_recv.at[gx],
            device_id=(lax.rem(gx + k, nx), gy), device_id_type=MESH,
        )

    def coeff_copy(side):
        dest = (right, left)[side]
        return pltpu.make_async_remote_copy(
            src_ref=coeff.at[1], dst_ref=coeff.at[2 * side], send_sem=coeff_send.at[side], recv_sem=coeff_recv.at[side],
            device_id=dest, device_id_type=MESH,
        )

    def start_terms(k, c):
        term_copy(k).start()
        return c

    def start_mids(k, c):
        for g in range(3):
            mid_copy(g, k).start()
        return c

    lax.fori_loop(1, ny, start_terms, 0)
    for c in halo:
        c.start()
    mid_copy(0, 0).start()
    mid_copy(2, 0).start()
    lax.fori_loop(1, ny, start_mids, 0)

    turn = eye(128)

    def transpose(s, c):
        x = src[pl.ds(s * SPITCH, 64), :].astype(bf16)
        sq[s] = nt(turn, x).astype(bf16)
        return c

    lax.fori_loop(0, leaves, transpose, 0, unroll=16)
    zero = jnp.zeros((32, 128), bf16)

    def near_chunk(k, c):
        def kernels(b, c):
            l = k * CHUNK + b
            t = tgt[pl.ds(l * TPITCH, 32), :].astype(bf16)
            w = jnp.concatenate([jnp.concatenate([t, zero], 1), jnp.concatenate([zero, t], 1)], 0)
            for n in range(8):
                both = mm(sq[slot_of(ids[n, l], first, leaves)], w)
                f = both[:, 128:]
                r = lax.rsqrt(both[:, :128])
                pairs_buf[b, pl.ds(n * 128, 128), :] = (f * r * (r * r)).astype(bf16)
            return c

        def apply(b, c):
            l = k * CHUNK + b
            values = [dens[slot_of(ids[n, l], first, leaves)] for n in range(8)]
            near[l] = mm(jnp.concatenate(values, 1), pairs_buf[b])
            return c

        lax.fori_loop(0, CHUNK, kernels, 0, unroll=8)
        lax.fori_loop(0, CHUNK, apply, 0, unroll=8)
        return c

    chunks = leaves // CHUNK
    cuts = (1, 3, 9, chunks - 1)

    def near_range(a, b):
        lax.fori_loop(a, b, near_chunk, 0)

    near_range(cuts[0], cuts[1])

    def wait_terms(k, c):
        other = lax.rem(gy + k, ny)
        pltpu.make_async_remote_copy(
            src_ref=term_all.at[other], dst_ref=term_all.at[other], send_sem=term_send.at[k],
            recv_sem=term_recv.at[other], device_id=(gx, other), device_id_type=MESH,
        ).wait_recv()
        return c

    lax.fori_loop(1, ny, wait_terms, 0)
    total = term_all[0]
    for u in range(1, ny):
        total = total + term_all[u]
    top_all[gx] = total.astype(bf16)

    def start_tops(k, c):
        top_copy(k).start()
        return c

    lax.fori_loop(1, nx, start_tops, 0)
    for side in range(2):
        coeff_copy(side).start()
    near_range(cuts[1], cuts[2])
    def wait_tops(k, c):
        other = lax.rem(gx + k, nx)
        pltpu.make_async_remote_copy(
            src_ref=top_all.at[other], dst_ref=top_all.at[other], send_sem=top_send.at[k],
            recv_sem=top_recv.at[other], device_id=(other, gy), device_id_type=MESH,
        ).wait_recv()
        return c

    def wait_mid(slot, k):
        pltpu.make_async_remote_copy(
            src_ref=mid_all.at[slot], dst_ref=mid_all.at[slot], send_sem=mid_send.at[0, k],
            recv_sem=mid_recv.at[slot], device_id=(gx, lax.rem(gy + 1, ny)), device_id_type=MESH,
        ).wait_recv()

    def wait_mids(k, c):
        other = lax.rem(gy + k, ny)
        for g in range(3):
            wait_mid(g * ny + other, k)
        return c

    lax.fori_loop(1, nx, wait_tops, 0)
    wait_mid(gy, 0)
    wait_mid(2 * ny + gy, 0)
    lax.fori_loop(1, ny, wait_mids, 0)
    for c in loads[6:12]:
        c.wait()

    root_field = jnp.zeros((32, 64), f32)
    for q in range(nx // BRANCH):
        root = jnp.zeros((32, 64), f32)
        for j in range(BRANCH):
            g = q * BRANCH + j
            root = root + nt(unfold(top_all[g]), group_up[g])
        root_field = root_field + nt(root.astype(bf16), root_row[q])
    top_field = nt(root_field.astype(bf16), group_down[0])
    for f in range(group_coupling.shape[1]):
        top_field = top_field + nt(unfold(top_all[group_far[0, f]]), group_coupling[0, f])
    mid_field = nt(top_field.astype(bf16), cluster_down[0])
    for f in range(cluster_coupling.shape[1]):
        u = jnp.clip(cluster_far[0, f] - (gx - 1) * ny, 0, 3 * ny - 1)
        mid_field = mid_field + nt(unfold(mid_all[u]), cluster_coupling[0, f])
    parent = jnp.concatenate([mid_field, jnp.zeros((32, 64), f32)], axis=1).astype(bf16)

    near_range(cuts[2], cuts[3])
    for c in halo:
        c.wait()
    dens[pl.ds(leaves + HALO - REACH, 2 * REACH)] = dens_halo[pl.ds(HALO - REACH, 2 * REACH)]
    for side in range(2):
        extent = jnp.maximum(
            extent, prepare(geo_halo.at[side], HALO, leaves + HALO * side, origin, src, None)
        )
    extent_out[...] = jnp.full(extent_out.shape, extent, f32)

    halo_copy = pltpu.make_async_copy(dens_halo, dens_halo_out, out_sem.at[0])
    halo_copy.start()
    geo_copy = pltpu.make_async_copy(geo_halo, geo_halo_out, out_sem.at[1])
    geo_copy.start()

    lax.fori_loop(leaves, leaves + 2 * HALO, transpose, 0, unroll=16)
    lax.fori_loop(0, 2, lambda k, c: near_chunk(k * (chunks - 1), c), 0)

    for side in range(2):
        coeff_copy(side).wait()

    def spread(p, c):
        for side in range(3):
            tile = coeff[side, p].astype(f32)
            turned = pltpu.roll(tile, 64, 1)
            dup[side * leaves + 2 * p] = jnp.where(low, tile, turned).astype(bf16)
            dup[side * leaves + 2 * p + 1] = jnp.where(low, turned, tile).astype(bf16)
        return c

    lax.fori_loop(0, pairs, spread, 0, unroll=8)
    dup[3 * leaves] = jnp.zeros((32, 128), bf16)

    def leaf_fields(l, c):
        lhs, mats = [], []
        for f in range(3):
            tiles = []
            for b in range(2):
                k = 2 * f + b
                s = jnp.where(k < count[l], far[k, l] - (first - leaves), 3 * leaves)
                tiles.append(dup[jnp.clip(s, 0, 3 * leaves)])
            lhs.append(jnp.where(low, tiles[0], tiles[1]))
            mats.append(coupling_relay[f, pl.ds(l, 64, RPITCH), :].astype(bf16))
        lhs.append(parent)
        mats.append(lift[l])
        field[l] = nt(jnp.concatenate(lhs, 1), jnp.concatenate(mats, 1)).astype(bf16)
        return c

    def panels(l, c):
        near[l] = near[l] + mm(field[l], panel_basis[l])
        return c

    lax.fori_loop(0, leaves, leaf_fields, 0, unroll=16)
    field_copy = pltpu.make_async_copy(field, field_out, out_sem.at[2])
    field_copy.start()
    loads[13].wait()
    third = leaves // 3
    total_copies = []
    for k in range(3):
        lax.fori_loop(k * third, (k + 1) * third, panels, 0, unroll=8)
        rows = pl.ds(k * third, third)
        total_copies.append(pltpu.make_async_copy(near.at[rows], total_out.at[rows], out_sem.at[3 + k]))
        total_copies[-1].start()

    def finish_y(k, c):
        term_copy(k).wait_send()
        for g in range(3):
            mid_copy(g, k).wait_send()
        return c

    def finish_x(k, c):
        top_copy(k).wait_send()
        return c

    lax.fori_loop(1, ny, finish_y, 0)
    mid_copy(0, 0).wait_send()
    mid_copy(2, 0).wait_send()
    lax.fori_loop(1, nx, finish_x, 0)
    for c in (halo_copy, geo_copy, field_copy, *total_copies):
        c.wait()


def finish_kernel(
    leaves, first_ref, extent, near_ids, total_hbm, field_hbm, basis_hbm, geo_hbm, geo_halo_hbm, dens_hbm, dens_halo_hbm,
    out_hbm,
    out, field, basis, geo, geo_halo, dens, in_sem, out_sem, slow_sem,
):
    first = first_ref[0]
    parts = 4
    size = leaves // parts
    rows = [pl.ds(k * size, size) for k in range(parts)]
    ins = [pltpu.make_async_copy(total_hbm.at[r], out.at[r], in_sem.at[k]) for k, r in enumerate(rows)]
    outs = [pltpu.make_async_copy(out.at[r], out_hbm.at[r], out_sem.at[k]) for k, r in enumerate(rows)]
    for c in ins:
        c.start()
    resolved = jnp.max(extent[...]) < FAR_LIMIT

    @pl.when(resolved)
    def _():
        for i, o in zip(ins, outs):
            i.wait()
            o.start()
        for o in outs:
            o.wait()

    @pl.when(jnp.logical_not(resolved))
    def _():
        for i in ins:
            i.wait()
        copies = [
            pltpu.make_async_copy(geo_hbm, geo, slow_sem.at[0]),
            pltpu.make_async_copy(geo_halo_hbm, geo_halo, slow_sem.at[1]),
            pltpu.make_async_copy(dens_hbm, dens.at[pl.ds(0, leaves)], slow_sem.at[2]),
            pltpu.make_async_copy(dens_halo_hbm, dens.at[pl.ds(leaves, 2 * HALO)], slow_sem.at[3]),
            pltpu.make_async_copy(field_hbm, field, slow_sem.at[4]),
            pltpu.make_async_copy(basis_hbm, basis, slow_sem.at[5]),
        ]
        for c in copies:
            c.start()
        for c in copies:
            c.wait()

        def leaf(l, c):
            out[l] = mm(field[l], basis[l])

            def one(n, c):
                s = slot_of(near_ids[n, l], first, leaves)
                rows = []
                for k in range(7):
                    local = geo[k, pl.ds(jnp.minimum(s, leaves - 1), 1), :]
                    sl = geo_halo[0, k, pl.ds(jnp.clip(s - leaves, 0, HALO - 1), 1), :]
                    sr = geo_halo[1, k, pl.ds(jnp.clip(s - leaves - HALO, 0, HALO - 1), 1), :]
                    rows.append(jnp.where(s < leaves, local, jnp.where(s < leaves + HALO, sl, sr)))
                rows.append(jnp.zeros((1, 128), f32))
                cols = jnp.concatenate(rows, axis=0).T
                off = [geo[k, pl.ds(l, 1), :] - cols[:, k : k + 1] for k in range(3)]
                area = cols[:, 6:7]
                wide = off[0] * off[0] + off[1] * off[1] + off[2] * off[2] + area
                facing = cols[:, 3:4] * off[0] + cols[:, 4:5] * off[1] + cols[:, 5:6] * off[2]
                kern = area * facing / (4.0 * math.pi * wide * jnp.sqrt(wide))
                out[l] += mm(dens[s], kern.astype(bf16))
                return c

            return lax.fori_loop(0, 8, one, c)

        lax.fori_loop(0, leaves, leaf, 0)
        for o in outs:
            o.start()
        for o in outs:
            o.wait()


def on_device(
    nx, ny, densities, geometry, near_ids, basis_in, basis_out, leaf_up, leaf_down, leaf_coupling, leaf_far, leaf_count,
    cluster_up, cluster_down, cluster_coupling, cluster_far, group_up, group_down, group_coupling, group_far,
    root_coupling,
):
    leaves = densities.shape[0]
    slots = leaves + 2 * HALO
    geo = jnp.transpose(geometry, (1, 0, 2))
    up = jnp.transpose(leaf_up, (1, 2, 0))
    down = jnp.transpose(leaf_down, (1, 2, 0))
    coupling = jnp.transpose(leaf_coupling, (1, 2, 3, 0))
    ids = near_ids.T
    far = leaf_far.T
    V = pl.BlockSpec(memory_space=pltpu.VMEM)
    S = pl.BlockSpec(memory_space=pltpu.SMEM)
    H = pl.BlockSpec(memory_space=pl.ANY)
    dma = pltpu.SemaphoreType.DMA
    shape = jax.ShapeDtypeStruct
    total, field, extent, dens_halo, geo_halo = pl.pallas_call(
        functools.partial(up_kernel, nx, ny, leaves),
        name="up",
        out_shape=(
            shape((leaves, 32, 128), f32),
            shape((leaves, 32, 64), bf16),
            shape((8, 128), f32),
            shape((2 * HALO, 32, 128), bf16),
            shape((2, 7, HALO, 128), f32),
        ),
        in_specs=[S] * 5 + [H] * 14,
        out_specs=(H, H, V, H, H),
        scratch_shapes=[
            pltpu.VMEM((7, leaves, 128), f32),
            pltpu.VMEM((slots, 32, 128), bf16),
            pltpu.VMEM((leaves, 64, 128), bf16),
            pltpu.VMEM((leaves, 64, 128), bf16),
            pltpu.VMEM((64, 64, leaves), bf16),
            pltpu.VMEM((64, 64, leaves), bf16),
            pltpu.VMEM((1, 64, 64), bf16),
            pltpu.VMEM((1, 64, 64), bf16),
            pltpu.VMEM(cluster_coupling.shape, bf16),
            pltpu.VMEM(group_up.shape, bf16),
            pltpu.VMEM((1, 64, 64), bf16),
            pltpu.VMEM(group_coupling.shape, bf16),
            pltpu.VMEM((2, 7, HALO, 128), f32),
            pltpu.VMEM((2 * HALO, 32, 128), bf16),
            pltpu.VMEM((slots * SPITCH, 128), f32),
            pltpu.VMEM((leaves * TPITCH, 128), f32),
            pltpu.VMEM((slots, 128, 64), bf16),
            pltpu.VMEM((64 * RPITCH, 128), f32),
            pltpu.VMEM(coupling.shape, bf16),
            pltpu.VMEM((3, 64 * RPITCH, 128), f32),
            pltpu.VMEM((leaves, 64, 128), bf16),
            pltpu.VMEM((3, leaves // 2, 32, 128), bf16),
            pltpu.VMEM((3 * leaves + 1, 32, 128), bf16),
            pltpu.VMEM((leaves, 32, 64), bf16),
            pltpu.VMEM((leaves // 2, 32, 256), bf16),
            pltpu.VMEM((3 * ny, 16, 128), bf16),
            pltpu.VMEM((ny, 16, 128), f32),
            pltpu.VMEM((nx, 16, 128), bf16),
            pltpu.VMEM((nx // BRANCH, 64, 64), bf16),
            pltpu.VMEM((CHUNK, 8 * 128, 128), bf16),
            pltpu.VMEM((leaves, 32, 128), f32),
            dma((14,)), dma((6,)), dma((4,)), dma((4,)), dma((2,)), dma((2,)), dma((3, ny)), dma((3 * ny,)),
            dma((ny,)), dma((ny,)), dma((nx,)), dma((nx,)),
        ],
        compiler_params=pltpu.CompilerParams(
            collective_id=0, has_side_effects=True, vmem_limit_bytes=VMEM_LIMIT
        ),
    )(
        ids, far, leaf_count, cluster_far, group_far, geo, densities, basis_in, up, down, cluster_up, cluster_down, cluster_coupling,
        group_up, group_down, group_coupling, root_coupling, coupling, basis_out,
    )
    first = ((lax.axis_index("gx") * ny + lax.axis_index("gy")) * leaves).reshape(1)
    return pl.pallas_call(
        functools.partial(finish_kernel, leaves),
        name="finish",
        out_shape=shape((leaves, 32, 128), f32),
        in_specs=[S, V, S] + [H] * 7,
        out_specs=H,
        scratch_shapes=[
            pltpu.VMEM((leaves, 32, 128), f32),
            pltpu.VMEM((leaves, 32, 64), bf16),
            pltpu.VMEM((leaves, 64, 128), bf16),
            pltpu.VMEM((7, leaves, 128), f32),
            pltpu.VMEM((2, 7, HALO, 128), f32),
            pltpu.VMEM((slots, 32, 128), bf16),
            dma((4,)), dma((4,)), dma((6,)),
        ],
        compiler_params=pltpu.CompilerParams(vmem_limit_bytes=VMEM_LIMIT),
    )(first, extent, ids, total, field, basis_out, geo, geo_halo, densities, dens_halo)


def solution(mesh):
    leaf = ("gx", "gy")
    return jax.shard_map(
        functools.partial(on_device, mesh.shape["gx"], mesh.shape["gy"]),
        mesh=mesh,
        in_specs=(
            P(leaf, None, None),
            P(leaf, None, None),
            P(leaf, None),
            P(leaf, None, None),
            P(leaf, None, None),
            P(leaf, None, None),
            P(leaf, None, None),
            P(leaf, None, None, None),
            P(leaf, None),
            P(leaf),
            P(leaf, None, None),
            P(leaf, None, None),
            P(leaf, None, None, None),
            P(leaf, None),
            P(),
            P("gx", None, None),
            P("gx", None, None, None),
            P("gx", None),
            P(),
        ),
        out_specs=P(leaf, None, None),
        check_vma=False,
    )
```
